32 devices in a mesh: tile: 16 (over z, y, core), inner: 2 (over x).
Axes of the slice: x: 2, y: 2, z: 4, core: 2. Of those that a mesh axis runs over, the one named last changes fastest.
Arguments:
- amplitudes: bfloat16 [512, 4096], P('tile', 'inner'), may hold values from -6 to 6
- left_factors: bfloat16 [1024, 4096], P('tile', 'inner'), may hold values from -0.1875 to 0.1875
- right_factors: bfloat16 [1024, 16384], P(None, 'tile'), may hold values from -0.1875 to 0.1875
- tile_pattern: int32 [8, 32], replicated, may hold values from 0 to 1, as said below
- occupied_shift: float32 [512], P('inner'), may hold values from 0.5 to 2
- virtual_shift: float32 [16384], P('tile'), may hold values from 0.5 to 5
Outputs:
- residual: float32 [512, 16384], P('inner', 'tile')
The draws below stay inside these ranges and needn't reach their ends.
Inputs may be any that keep to these rules, and one draw needn't show every extreme that they name: `tile_pattern`: 1 where the tiles interact, 0 where their integrals are dropped.
All inputs are finite; a program needn't handle non-finite values.
Results may differ from the reference program's by a relative error of at most 0.0029.
Values may be sent and summed in bfloat16 or wider, within the bound.
No kernel may reach another device: no remote copies, remote signals or barrier semaphores. Data moves between devices by JAX's collectives and lax.ppermute only.
A program may use at most 64 MiB of HBM per device.

```python
import math
import jax
import jax.numpy as jnp
from jax import lax

NAUX = 1024
TILE = 512
ROWS = 512
QP = 4096
PP = 16384


def draw_tile_pattern(key, part):
    level_key, cell_key = jax.random.split(jax.random.fold_in(key, 7))
    levels = jax.random.randint(level_key, (1, PP // TILE), 0, 4)
    limits = jnp.array([3, 6, 9, 16], jnp.int32)[levels]
    cells = jax.random.randint(cell_key, (QP // TILE, PP // TILE), 0, 24)
    return (cells < limits).astype(jnp.int32)


def block_levels(key, extent, shards, smallest, largest):
    level, own = 1.0, jax.random.fold_in(key, 6)
    for position, shards_of in shards:
        steps = jnp.exp(jax.random.uniform(jax.random.fold_in(own, position), (shards_of,), jnp.float32, smallest / len(shards), largest / len(shards)))
        level = level * jnp.repeat(steps, extent[position] // shards_of).reshape([-1 if axis == position else 1 for axis in range(len(extent))])
    return level


def normal_values(key, dims, spread, reach, pieces=(), kind=jnp.bfloat16):
    result = spread * jax.random.normal(key, dims, jnp.float32)
    if pieces:
        result = result * block_levels(key, dims, pieces, -0.22, 0.18)
    return jnp.clip(result, -reach, reach).astype(kind)


def setup_inputs(seed: int = 0) -> dict:
    arg_keys = jax.random.split(jax.random.key(seed), 7)
    amplitudes = normal_values(arg_keys[0], (ROWS, QP), 1.0, 6.0, ((0, 16), (1, 2)))
    left_factors = normal_values(arg_keys[1], (NAUX, QP), NAUX ** -0.5, 0.1875, ((0, 16), (1, 2)))
    right_factors = normal_values(arg_keys[2], (NAUX, PP), NAUX ** -0.5, 0.1875, ((1, 16),))
    tile_pattern = draw_tile_pattern(jax.random.fold_in(arg_keys[6], 71), 0)
    occupied_shift = jnp.clip(jnp.exp(math.log(2.0) - 1.3862944 * jax.random.uniform(arg_keys[4], (ROWS,), jnp.float32) ** block_levels(arg_keys[4], (ROWS,), ((0, 2),), -0.2, 0.2)), 0.5, 2.0)
    virtual_shift = jnp.clip(jnp.exp(math.log(5.0) - 2.3025851 * jax.random.uniform(arg_keys[5], (PP,), jnp.float32) ** block_levels(arg_keys[5], (PP,), ((0, 16),), -0.2, 0.2)), 0.5, 5.0)
    return dict(amplitudes=amplitudes, left_factors=left_factors, right_factors=right_factors, tile_pattern=tile_pattern, occupied_shift=occupied_shift, virtual_shift=virtual_shift)


def reference(amplitudes, left_factors, right_factors, tile_pattern, occupied_shift, virtual_shift):
    left_tiles = QP // TILE
    right_tiles = PP // TILE

    def column(right_index):
        right_index = right_index.astype(jnp.int32)
        right_cols = lax.dynamic_slice_in_dim(right_factors, right_index * TILE, TILE, 1)

        def visit_tile(left_index, totals):
            left_index = jnp.asarray(left_index).astype(jnp.int32)

            def include(current):
                left_cols = lax.dynamic_slice_in_dim(left_factors, left_index * TILE, TILE, 1)
                integral = lax.dot_general(left_cols, right_cols, (((0,), (0,)), ((), ())), preferred_element_type=jnp.float32).astype(jnp.bfloat16)
                amplitude_tile = lax.dynamic_slice_in_dim(amplitudes, left_index * TILE, TILE, 1)
                return current + jnp.dot(amplitude_tile, integral, preferred_element_type=jnp.float32)

            return lax.cond(tile_pattern[left_index, right_index] != 0, include, lambda current: current, totals)

        return lax.fori_loop(0, left_tiles, visit_tile, jnp.zeros((ROWS, TILE), jnp.float32))

    blocks = lax.map(column, jnp.arange(right_tiles, dtype=jnp.int32))
    ladder = jnp.transpose(blocks, (1, 0, 2)).reshape(ROWS, PP)
    return ladder / (occupied_shift[:, None] + virtual_shift[None, :])
```

```python
import functools

import jax
import jax.numpy as jnp
from jax import lax
from jax.experimental import pallas as pl
from jax.experimental.pallas import tpu as pltpu
from jax.sharding import PartitionSpec as P

TILE = 512
VMEM = pl.BlockSpec(memory_space=pltpu.VMEM)
SMEM = pl.BlockSpec(memory_space=pltpu.SMEM)


def products_kernel(z_size, inner_size, place, *refs):
    a_refs, l_refs = refs[:z_size], refs[z_size : z_size + 4]
    outs = refs[z_size + 4 : z_size + 4 + inner_size]
    a_all, l_all = refs[z_size + 4 + inner_size :]
    z, y, core, inner = place[0], place[1], place[2], place[3]
    row_block, width = a_refs[0].shape
    col_block = l_refs[0].shape[0]
    for q, ref in enumerate(a_refs):
        a_all[pl.ds(pl.multiple_of((z ^ q) * row_block, row_block), row_block), :] = ref[...].astype(a_all.dtype)
    for q, ref in enumerate(l_refs):
        where = ((y ^ (q // 2)) * 2 + (core ^ (q % 2))) * col_block
        l_all[pl.ds(pl.multiple_of(where, col_block), col_block), :] = ref[...]
    group = z_size // inner_size * row_block
    for p, out in enumerate(outs):
        start = pl.multiple_of((inner ^ p) * group, group)
        for c in range(width // TILE):
            cols = slice(c * TILE, (c + 1) * TILE)
            left = a_all[pl.ds(start, group), cols].astype(jnp.bfloat16)
            out[c] = lax.dot_general(
                left, l_all[:, cols], (((1,), (1,)), ((), ())), preferred_element_type=jnp.float32
            ).astype(out.dtype)


def totals_kernel(inner_size, chips, right_tiles, place, pattern, *refs):
    mine, other = refs[:inner_size], refs[inner_size : 2 * inner_size]
    outs = refs[2 * inner_size :]
    chip, core, inner = place[0], place[1], place[2]
    left_tiles, rows, _ = mine[0].shape
    for m in range(chips):
        first = ((chip ^ m) * 2 + core) * right_tiles
        for d in range(right_tiles):
            for rel, source in enumerate((mine, other)):
                total = None
                for p, ref in enumerate(source):
                    for c in range(left_tiles):
                        on = pattern[(inner ^ p) * left_tiles + c, first + d] != 0
                        term = jnp.where(on, 1.0, 0.0) * ref[c].astype(jnp.float32)
                        total = term if total is None else total + term
                outs[m][d, rel * rows : (rel + 1) * rows, :] = total.astype(jnp.bfloat16)


def residual_kernel(chips, z_groups, place, *refs):
    t_refs = refs[:chips]
    right, occupied, virtual, out = refs[chips:]
    z, y, core = place[0], place[1], place[2]
    right_tiles, rows, depth = t_refs[0].shape
    row_block = rows // (2 * z_groups)
    for d in range(right_tiles):
        cols = slice(d * TILE, (d + 1) * TILE)
        total = None
        for q in range(chips // 2):
            left = jnp.concatenate([t_refs[2 * q][d], t_refs[2 * q + 1][d]], axis=0)
            start = pl.multiple_of((z ^ q) * depth, depth)
            term = jnp.dot(left, right[pl.ds(start, depth), cols], preferred_element_type=jnp.float32)
            total = term if total is None else total + term
        for rel_y in range(2):
            for rel in range(2):
                for s in range(z_groups):
                    at = ((s * 2 + (y ^ rel_y)) * 2 + (core ^ rel)) * row_block
                    at = pl.multiple_of(at, row_block)
                    source = rel_y * rows + rel * z_groups * row_block + s * row_block
                    shift = occupied[pl.ds(at, row_block), :] + virtual[:, cols]
                    out[pl.ds(at, row_block), cols] = total[source : source + row_block, :] / shift


def solution(mesh):
    tiles, inner_size = mesh.shape["tile"], mesh.shape["inner"]
    z_size, chips = tiles // 4, tiles // 2
    params = pltpu.CompilerParams(vmem_limit_bytes=48 * 1024 * 1024)

    def swap(value, q, axis="tile", size=tiles):
        return lax.ppermute(value, axis, [(t, t ^ q) for t in range(size)])

    def on_device(amplitudes, left_factors, right_factors, tile_pattern, occupied_shift, virtual_shift):
        t = lax.axis_index("tile")
        inner = lax.axis_index("inner")
        z, y, core = t // 4, lax.rem(t // 2, 2), lax.rem(t, 2)
        row_block, width = amplitudes.shape
        col_block = left_factors.shape[0]
        out_width = right_factors.shape[1]
        left_tiles, right_tiles = width // TILE, out_width // TILE
        z_groups = z_size // inner_size
        rows, depth = z_groups * row_block, 4 * col_block

        by_y = swap(left_factors, 2)
        amps = [amplitudes] + [swap(amplitudes, 4 * q) for q in range(1, z_size)]
        by_core = swap(left_factors, 1)
        by_both = swap(by_y, 1)

        packed = jnp.bfloat16 if row_block % 16 == 0 else jnp.float32
        products = pl.pallas_call(
            functools.partial(products_kernel, z_size, inner_size),
            out_shape=[
                jax.ShapeDtypeStruct((left_tiles, rows, depth), jnp.float32 if p == 0 else jnp.bfloat16)
                for p in range(inner_size)
            ],
            in_specs=[SMEM] + [VMEM] * (z_size + 4),
            out_specs=[VMEM] * inner_size,
            scratch_shapes=[
                pltpu.VMEM((z_size * row_block, width), packed),
                pltpu.VMEM((depth, width), jnp.bfloat16),
            ],
            compiler_params=params,
            cost_estimate=pl.CostEstimate(
                flops=2 * z_size * row_block * width * depth, bytes_accessed=2 << 20, transcendentals=0
            ),
            name="products",
        )(jnp.stack([z, y, core, inner]).astype(jnp.int32), *amps, left_factors, by_core, by_y, by_both)

        mine = [products[0]] + [swap(products[p], p, "inner", inner_size) for p in range(1, inner_size)]
        other = [swap(part, 1) for part in mine]

        totals = pl.pallas_call(
            functools.partial(totals_kernel, inner_size, chips, right_tiles),
            out_shape=[jax.ShapeDtypeStruct((right_tiles, 2 * rows, depth), jnp.bfloat16)] * chips,
            in_specs=[SMEM, SMEM] + [VMEM] * (2 * inner_size),
            out_specs=[VMEM] * chips,
            compiler_params=params,
            cost_estimate=pl.CostEstimate(flops=1 << 24, bytes_accessed=2 << 20, transcendentals=0),
            name="totals",
        )(jnp.stack([t // 2, core, inner]).astype(jnp.int32), tile_pattern, *mine, *other)

        arrived = [totals[0]] + [swap(totals[m], 2 * m) for m in range(1, chips)]

        return pl.pallas_call(
            functools.partial(residual_kernel, chips, z_groups),
            out_shape=jax.ShapeDtypeStruct((occupied_shift.shape[0], out_width), jnp.float32),
            in_specs=[SMEM] + [VMEM] * (chips + 3),
            out_specs=VMEM,
            compiler_params=params,
            cost_estimate=pl.CostEstimate(
                flops=2 * occupied_shift.shape[0] * out_width * right_factors.shape[0],
                bytes_accessed=4 << 20,
                transcendentals=0,
            ),
            name="residual",
        )(
            jnp.stack([z, y, core]).astype(jnp.int32),
            *arrived,
            right_factors,
            occupied_shift.reshape(-1, 1),
            virtual_shift.reshape(1, -1),
        )

    placed = (P("tile", "inner"), P("tile", "inner"), P(None, "tile"), P(), P("inner"), P("tile"))
    return jax.shard_map(
        on_device, mesh=mesh, in_specs=placed, out_specs=P("inner", "tile"), check_vma=False
    )
```

```python
import functools

import jax
import jax.numpy as jnp
from jax import lax
from jax.experimental import pallas as pl
from jax.experimental.pallas import tpu as pltpu
from jax.sharding import PartitionSpec as P


TILE = 512
VMEM = pl.BlockSpec(memory_space=pltpu.VMEM)
SMEM = pl.BlockSpec(memory_space=pltpu.SMEM)
ANY = pl.BlockSpec(memory_space=pl.ANY)


def keep_kernel(*refs):
    half = len(refs) // 2
    for source, target in zip(refs[:half], refs[half:]):
        target[...] = source[...]


def products_kernel(z_size, inner_size, place, *refs):
    a_refs, l_refs = refs[:z_size], refs[z_size : z_size + 4]
    outs = refs[z_size + 4 : z_size + 4 + inner_size]
    a_all, l_all = refs[z_size + 4 + inner_size :]
    z, y, core, inner = place[0], place[1], place[2], place[3]
    row_block, width = a_refs[0].shape
    col_block = l_refs[0].shape[0]
    for q, ref in enumerate(a_refs):
        a_all[pl.ds(pl.multiple_of((z ^ q) * row_block, row_block), row_block), :] = ref[...].astype(a_all.dtype)
    for q, ref in enumerate(l_refs):
        where = ((y ^ (q // 2)) * 2 + (core ^ (q % 2))) * col_block
        l_all[pl.ds(pl.multiple_of(where, col_block), col_block), :] = ref[...]
    group = z_size // inner_size * row_block
    for p, out in enumerate(outs):
        start = pl.multiple_of((inner ^ p) * group, group)
        for c in range(width // TILE):
            cols = slice(c * TILE, (c + 1) * TILE)
            left = a_all[pl.ds(start, group), cols].astype(jnp.bfloat16)
            out[c] = lax.dot_general(
                left, l_all[:, cols], (((1,), (1,)), ((), ())), preferred_element_type=jnp.float32
            ).astype(out.dtype)


def totals_kernel(inner_size, chips, right_tiles, place, *refs):
    mine, other = refs[:inner_size], refs[inner_size : 2 * inner_size]
    outs = refs[2 * inner_size :]
    z, y, core, inner = place[0], place[1], place[2], place[3]
    chip = z * 2 + y
    columns = chips * 2 * right_tiles
    left_tiles, rows, _ = mine[0].shape
    for m in range(chips):
        first = ((chip ^ m) * 2 + core) * right_tiles
        for d in range(right_tiles):
            for rel, source in enumerate((mine, other)):
                total = None
                for p, ref in enumerate(source):
                    for c in range(left_tiles):
                        on = place[4 + ((inner ^ p) * left_tiles + c) * columns + first + d] != 0
                        term = jnp.where(on, 1.0, 0.0) * ref[c].astype(jnp.float32)
                        total = term if total is None else total + term
                outs[m][d, rel * rows : (rel + 1) * rows, :] = total.astype(jnp.bfloat16)


def residual_kernel(chips, z_groups, place, *refs):
    t_refs = refs[:chips]
    right, occupied, virtual_hbm, out, virtual, sem = refs[chips:]
    fetch = pltpu.make_async_copy(virtual_hbm, virtual, sem)
    fetch.start()
    z, y, core = place[0], place[1], place[2]
    right_tiles, rows, depth = t_refs[0].shape
    row_block = rows // (2 * z_groups)
    for d in range(right_tiles):
        cols = slice(d * TILE, (d + 1) * TILE)
        total = None
        for q in range(chips // 2):
            left = jnp.concatenate([t_refs[2 * q][d], t_refs[2 * q + 1][d]], axis=0)
            start = pl.multiple_of((z ^ q) * depth, depth)
            term = jnp.dot(left, right[pl.ds(start, depth), cols], preferred_element_type=jnp.float32)
            total = term if total is None else total + term
        if d == 0:
            fetch.wait()
        for rel_y in range(2):
            for rel in range(2):
                for s in range(z_groups):
                    at = ((s * 2 + (y ^ rel_y)) * 2 + (core ^ rel)) * row_block
                    at = pl.multiple_of(at, row_block)
                    source = rel_y * rows + rel * z_groups * row_block + s * row_block
                    shift = occupied[pl.ds(at, row_block), :] + virtual[:, cols]
                    out[pl.ds(at, row_block), cols] = total[source : source + row_block, :] / shift


def solution(mesh):
    tiles, inner_size = mesh.shape["tile"], mesh.shape["inner"]
    z_size, chips = tiles // 4, tiles // 2
    params = pltpu.CompilerParams(vmem_limit_bytes=20 * 1024 * 1024)

    def swap(value, q, axis="tile", size=tiles):
        return lax.ppermute(value, axis, [(t, t ^ q) for t in range(size)])

    def on_device(amplitudes, left_factors, right_factors, tile_pattern, occupied_shift, virtual_shift):
        t = lax.axis_index("tile")
        inner = lax.axis_index("inner")
        z, y, core = t // 4, lax.rem(t // 2, 2), lax.rem(t, 2)
        row_block, width = amplitudes.shape
        col_block = left_factors.shape[0]
        out_width = right_factors.shape[1]
        left_tiles, right_tiles = width // TILE, out_width // TILE
        z_groups = z_size // inner_size
        rows, depth = z_groups * row_block, 4 * col_block

        by_y = swap(left_factors, 2)
        by_core = swap(left_factors, 1)
        by_both = swap(by_y, 1)
        moved = {q: swap(amplitudes, 4 * q) for q in range(1, z_size)}
        place = jnp.stack([z, y, core, inner]).astype(jnp.int32)
        place = jnp.concatenate([place, (tile_pattern != 0).astype(jnp.int32).reshape(-1)])
        kept = pl.pallas_call(
            keep_kernel,
            out_shape=[pltpu.VMEM(v.shape, v.dtype) for v in (amplitudes, left_factors)],
            in_specs=[VMEM] * 2,
            out_specs=[VMEM] * 2,
            cost_estimate=pl.CostEstimate(flops=0, bytes_accessed=1 << 20, transcendentals=0),
            name="keep",
        )(amplitudes, left_factors)
        amps = [kept[0]] + [moved[q] for q in range(1, z_size)]

        packed = jnp.bfloat16 if row_block % 16 == 0 else jnp.float32
        products = pl.pallas_call(
            functools.partial(products_kernel, z_size, inner_size),
            out_shape=[
                jax.ShapeDtypeStruct((left_tiles, rows, depth), jnp.float32 if p == 0 else jnp.bfloat16)
                for p in range(inner_size)
            ],
            in_specs=[SMEM] + [VMEM] * (z_size + 4),
            out_specs=[VMEM] * inner_size,
            scratch_shapes=[
                pltpu.VMEM((z_size * row_block, width), packed),
                pltpu.VMEM((depth, width), jnp.bfloat16),
            ],
            compiler_params=params,
            cost_estimate=pl.CostEstimate(
                flops=2 * z_size * row_block * width * depth, bytes_accessed=2 << 20, transcendentals=0
            ),
            name="products",
        )(place, *amps, kept[1], by_core, by_y, by_both)

        mine = [products[0]] + [swap(products[p], p, "inner", inner_size) for p in range(1, inner_size)]
        other = [swap(part, 1) for part in mine]

        totals = pl.pallas_call(
            functools.partial(totals_kernel, inner_size, chips, right_tiles),
            out_shape=[jax.ShapeDtypeStruct((right_tiles, 2 * rows, depth), jnp.bfloat16)] * chips,
            in_specs=[SMEM] + [VMEM] * (2 * inner_size),
            out_specs=[VMEM] * chips,
            compiler_params=params,
            cost_estimate=pl.CostEstimate(flops=1 << 24, bytes_accessed=2 << 20, transcendentals=0),
            name="totals",
        )(place, *mine, *other)

        arrived = [totals[0]] + [swap(totals[m], 2 * m) for m in range(1, chips)]

        return pl.pallas_call(
            functools.partial(residual_kernel, chips, z_groups),
            out_shape=jax.ShapeDtypeStruct((occupied_shift.shape[0], out_width), jnp.float32),
            in_specs=[SMEM] + [VMEM] * (chips + 2) + [ANY],
            out_specs=VMEM,
            scratch_shapes=[pltpu.VMEM((1, out_width), jnp.float32), pltpu.SemaphoreType.DMA(())],
            compiler_params=params,
            cost_estimate=pl.CostEstimate(
                flops=2 * occupied_shift.shape[0] * out_width * right_factors.shape[0],
                bytes_accessed=4 << 20,
                transcendentals=0,
            ),
            name="residual",
        )(
            place,
            *arrived,
            right_factors,
            occupied_shift.reshape(-1, 1),
            virtual_shift.reshape(1, -1),
        )

    placed = (P("tile", "inner"), P("tile", "inner"), P(None, "tile"), P(), P("inner"), P("tile"))

    return jax.shard_map(on_device, mesh=mesh, in_specs=placed, out_specs=P("inner", "tile"), check_vma=False)
```

```python
import functools

import jax
import jax.numpy as jnp
from jax import lax
from jax.experimental import pallas as pl
from jax.experimental.pallas import tpu as pltpu
from jax.sharding import PartitionSpec as P


TILE = 512
VMEM = pl.BlockSpec(memory_space=pltpu.VMEM)
SMEM = pl.BlockSpec(memory_space=pltpu.SMEM)
ANY = pl.BlockSpec(memory_space=pl.ANY)
PARAMS = pltpu.CompilerParams(vmem_limit_bytes=20 * 1024 * 1024)


def cost(flops, moved):
    return pl.CostEstimate(flops=int(flops), bytes_accessed=int(moved), transcendentals=0)


def keep_kernel(*refs):
    half = len(refs) // 2
    for source, target in zip(refs[:half], refs[half:]):
        target[...] = source[...]


def multiply(parts, place, a_refs, l_all, outs, a_all, result):
    z, inner = place[0], place[3]
    rows, width = a_refs[0].shape
    for r, ref in enumerate(a_refs):
        a_all[r * rows : (r + 1) * rows, :] = ref[...].astype(a_all.dtype)
    for c in range(width // TILE):
        cols = slice(c * TILE, (c + 1) * TILE)
        result[...] = lax.dot_general(
            a_all[:, cols].astype(jnp.bfloat16),
            l_all[:, cols],
            (((1,), (1,)), ((), ())),
            preferred_element_type=jnp.float32,
        )
        for p, out in enumerate(outs):
            start = pl.multiple_of((inner ^ p ^ (z // parts)) * rows, rows)
            out[c] = result[pl.ds(start, rows), :].astype(out.dtype)


def first_products_kernel(inner_size, parts, place, *refs):
    a_refs, l_refs = refs[:inner_size], refs[inner_size : inner_size + 4]
    outs = refs[inner_size + 4 : 2 * inner_size + 4]
    l_all, a_all, result = refs[2 * inner_size + 4 :]
    y, core = place[1], place[2]
    block = l_refs[0].shape[0]
    for q, ref in enumerate(l_refs):
        where = ((y ^ (q // 2)) * 2 + (core ^ (q % 2))) * block
        l_all[pl.ds(pl.multiple_of(where, block), block), :] = ref[...]
    multiply(parts, place, a_refs, l_all, outs, a_all, result)


def next_products_kernel(inner_size, parts, place, *refs):
    a_refs, l_all = refs[:inner_size], refs[inner_size]
    outs = refs[inner_size + 1 : 2 * inner_size + 1]
    a_all, result = refs[2 * inner_size + 1 :]
    multiply(parts, place, a_refs, l_all, outs, a_all, result)


def totals_kernel(inner_size, parts, targets, columns, right_tiles, place, *refs):
    count = 2 * inner_size * parts
    sources, outs = refs[:count], refs[count:]
    z, y, core, inner = place[0], place[1], place[2], place[3]
    chip = z * 2 + y
    left_tiles, rows, _ = sources[0].shape
    for m, out in zip(targets, outs):
        first = ((chip ^ m) * 2 + core) * right_tiles
        for d in range(right_tiles):
            for s in range(parts):
                blocks = []
                for rel in range(2):
                    total = None
                    for p in range(inner_size):
                        ref = sources[(s * 2 + rel) * inner_size + p]
                        for c in range(left_tiles):
                            on = place[4 + ((inner ^ p) * left_tiles + c) * columns + first + d] != 0
                            term = jnp.where(on, 1.0, 0.0) * ref[c].astype(jnp.float32)
                            total = term if total is None else total + term
                    blocks.append(total)
                at = slice(s * 2 * rows, (s + 1) * 2 * rows)
                out[d, at, :] = jnp.concatenate(blocks, axis=0).astype(jnp.bfloat16)


def residual_kernel(chips, parts, rows, place, *refs):
    half = chips // 2
    near, far = refs[:half], refs[half : half + parts * half]
    right, occupied, virtual_hbm, out, virtual, sem = refs[half + parts * half :]
    fetch = pltpu.make_async_copy(virtual_hbm, virtual, sem)
    fetch.start()
    z, y, core = place[0], place[1], place[2]
    right_tiles, _, depth = near[0].shape
    low = lax.rem(z, parts)

    def block(m, s, d):
        if m < half:
            return near[m][d, s * 2 * rows : (s + 1) * 2 * rows, :]
        return far[s * half + m - half][d]

    for d in range(right_tiles):
        cols = slice(d * TILE, (d + 1) * TILE)
        total = None
        for q in range(half):
            pieces = [block(2 * q + rel_y, o ^ (q % parts), d) for o in range(parts) for rel_y in range(2)]
            start = pl.multiple_of((z ^ q) * depth, depth)
            term = jnp.dot(
                jnp.concatenate(pieces, axis=0),
                right[pl.ds(start, depth), cols],
                preferred_element_type=jnp.float32,
            )
            total = term if total is None else total + term
        if d == 0:
            fetch.wait()
        source = 0
        for o in range(parts):
            for rel_y in range(2):
                for rel in range(2):
                    at = (((low ^ o) * 2 + (y ^ rel_y)) * 2 + (core ^ rel)) * rows
                    at = pl.multiple_of(at, rows)
                    shift = occupied[pl.ds(at, rows), :] + virtual[:, cols]
                    out[pl.ds(at, rows), cols] = total[source : source + rows, :] / shift
                    source += rows


def solution(mesh):
    tiles, inner_size = mesh.shape["tile"], mesh.shape["inner"]
    z_size, chips = tiles // 4, tiles // 2
    parts, half = z_size // inner_size, chips // 2

    def swap(value, q, axis="tile", size=tiles):
        return lax.ppermute(value, axis, [(t, t ^ q) for t in range(size)])

    def call(kernel, operands, in_specs, out_shape, scratch=(), flops=0, moved=1 << 20):
        many = isinstance(out_shape, list)
        return pl.pallas_call(
            kernel,
            out_shape=out_shape,
            in_specs=in_specs,
            out_specs=[VMEM] * len(out_shape) if many else VMEM,
            scratch_shapes=list(scratch),
            compiler_params=PARAMS,
            cost_estimate=cost(flops, moved),
        )(*operands)

    def on_device(amplitudes, left_factors, right_factors, tile_pattern, occupied_shift, virtual_shift):
        t = lax.axis_index("tile")
        inner = lax.axis_index("inner")
        z, y, core = t // 4, lax.rem(t // 2, 2), lax.rem(t, 2)
        rows, width = amplitudes.shape
        block = left_factors.shape[0]
        out_width = right_factors.shape[1]
        left_tiles, right_tiles = width // TILE, out_width // TILE
        depth = 4 * block

        place = jnp.stack([z, y, core, inner]).astype(jnp.int32)
        place = jnp.concatenate([place, (tile_pattern != 0).astype(jnp.int32).reshape(-1)])
        kept = call(
            keep_kernel,
            (amplitudes, left_factors),
            [VMEM] * 2,
            [pltpu.VMEM(v.shape, v.dtype) for v in (amplitudes, left_factors)],
        )
        by_y = swap(left_factors, 2)
        lefts = [kept[1], swap(left_factors, 1), by_y, swap(by_y, 1)]
        amps = {q: swap(amplitudes, 4 * q) for q in range(1, z_size)}
        amps[0] = kept[0]

        packed = jnp.bfloat16 if rows % 16 == 0 else jnp.float32
        scratch = [
            pltpu.VMEM((inner_size * rows, width), packed),
            pltpu.VMEM((inner_size * rows, depth), jnp.float32),
        ]
        shapes = [
            jax.ShapeDtypeStruct((left_tiles, rows, depth), jnp.float32 if p == 0 else jnp.bfloat16)
            for p in range(inner_size)
        ]
        flops = 2 * inner_size * rows * width * depth
        sources = []
        for s in range(parts):
            blocks = [amps[r * parts + s] for r in range(inner_size)]
            if s == 0:
                *products, left_all = call(
                    functools.partial(first_products_kernel, inner_size, parts),
                    (place, *blocks, *lefts),
                    [SMEM] + [VMEM] * (inner_size + 4),
                    shapes + [pltpu.VMEM((depth, width), jnp.bfloat16)],
                    scratch,
                    flops,
                )
            else:
                products = call(
                    functools.partial(next_products_kernel, inner_size, parts),
                    (place, *blocks, left_all),
                    [SMEM] + [VMEM] * (inner_size + 1),
                    shapes,
                    scratch,
                    flops,
                )
            mine = [products[0]]
            mine += [swap(products[p], p, "inner", inner_size) for p in range(1, inner_size)]
            other = [swap(part, 1) for part in mine]
            sources.append(mine + other)

        def totals(chosen, targets):
            operands = [ref for s in chosen for ref in sources[s]]
            return call(
                functools.partial(
                    totals_kernel, inner_size, len(chosen), targets, tile_pattern.shape[1], right_tiles
                ),
                (place, *operands),
                [SMEM] + [VMEM] * len(operands),
                [jax.ShapeDtypeStruct((right_tiles, len(chosen) * 2 * rows, depth), jnp.bfloat16)] * len(targets),
            )

        far = []
        for s in range(parts):
            made = totals([s], range(half, chips))
            far += [swap(made[m - half], 2 * m) for m in range(half, chips)]
        made = totals(range(parts), range(half))
        near = [made[0]] + [swap(made[m], 2 * m) for m in range(1, half)]

        return call(
            functools.partial(residual_kernel, chips, parts, rows),
            (
                place,
                *near,
                *far,
                right_factors,
                occupied_shift.reshape(-1, 1),
                virtual_shift.reshape(1, -1),
            ),
            [SMEM] + [VMEM] * (half + parts * half + 2) + [ANY],
            jax.ShapeDtypeStruct((occupied_shift.shape[0], out_width), jnp.float32),
            [pltpu.VMEM((1, out_width), jnp.float32), pltpu.SemaphoreType.DMA(())],
            2 * occupied_shift.shape[0] * out_width * right_factors.shape[0],
            4 << 20,
        )


    placed = (P("tile", "inner"), P("tile", "inner"), P(None, "tile"), P(), P("inner"), P("tile"))
    return jax.shard_map(on_device, mesh=mesh, in_specs=placed, out_specs=P("inner", "tile"), check_vma=False)
```

```python
import functools

import jax
import jax.numpy as jnp
from jax import lax
from jax.experimental import pallas as pl
from jax.experimental.pallas import tpu as pltpu
from jax.sharding import PartitionSpec as P


TILE = 512
VMEM = pl.BlockSpec(memory_space=pltpu.VMEM)
SMEM = pl.BlockSpec(memory_space=pltpu.SMEM)
ANY = pl.BlockSpec(memory_space=pl.ANY)
PARAMS = pltpu.CompilerParams(vmem_limit_bytes=20 * 1024 * 1024)


def cost(flops, moved):
    return pl.CostEstimate(flops=int(flops), bytes_accessed=int(moved), transcendentals=0)


def keep_kernel(amplitudes, left, kept):
    rows = amplitudes.shape[0]
    kept[:rows, :] = amplitudes[...]
    kept[rows:, :] = left[...]


def place():
    t = lax.axis_index("tile")
    return t // 4, lax.rem(t // 2, 2), lax.rem(t, 2), lax.axis_index("inner")


def multiply(parts, a_refs, l_all, outs, a_all, result):
    z, _, _, inner = place()
    rows, width = a_refs[0].shape
    for r, ref in enumerate(a_refs):
        a_all[r * rows : (r + 1) * rows, :] = ref[...].astype(a_all.dtype)
    for c in range(width // TILE):
        cols = slice(c * TILE, (c + 1) * TILE)
        result[...] = lax.dot_general(
            a_all[:, cols].astype(jnp.bfloat16),
            l_all[:, cols],
            (((1,), (1,)), ((), ())),
            preferred_element_type=jnp.float32,
        )
        for p in range(len(outs) // 2):
            start = pl.multiple_of((inner ^ p ^ (z // parts)) * rows, rows)
            value = result[pl.ds(start, rows), :]
            outs[2 * p][c] = value
            outs[2 * p + 1][c] = value.astype(jnp.bfloat16)


def first_products_kernel(inner_size, parts, kept, *refs):
    a_refs, l_refs = refs[: inner_size - 1], refs[inner_size - 1 : inner_size + 2]
    outs = refs[inner_size + 2 : 3 * inner_size + 2]
    l_all, a_all, result = refs[3 * inner_size + 2 :]
    _, y, core, _ = place()
    block = l_refs[0].shape[0]
    rows = kept.shape[0] - block
    for q, ref in enumerate((kept.at[rows:, :],) + l_refs):
        where = ((y ^ (q // 2)) * 2 + (core ^ (q % 2))) * block
        l_all[pl.ds(pl.multiple_of(where, block), block), :] = ref[...]
    multiply(parts, (kept.at[:rows, :],) + a_refs, l_all, outs, a_all, result)


def next_products_kernel(inner_size, parts, *refs):
    a_refs, l_all = refs[:inner_size], refs[inner_size]
    outs = refs[inner_size + 1 : 3 * inner_size + 1]
    a_all, result = refs[3 * inner_size + 1 :]
    multiply(parts, a_refs, l_all, outs, a_all, result)


def totals_kernel(inner_size, right_tiles, mask, *refs):
    count = 4 * inner_size
    sources, outs = refs[:count], refs[count:]
    z, y, core, inner = place()
    chip = z * 2 + y
    left_tiles, _, depth = sources[0].shape
    lanes = mask.shape[2]
    for m, out in enumerate(outs):
        first = ((chip ^ m) * 2 + core) * right_tiles
        for d in range(right_tiles):
            for b in range(2):
                blocks = []
                for rel in range(2):
                    total = None
                    for p in range(inner_size):
                        ref = sources[(b * 2 + rel) * inner_size + p]
                        for c in range(left_tiles):
                            on = mask[(inner ^ p) * left_tiles + c, pl.ds(first + d, 1), :]
                            on = jnp.concatenate([on] * (depth // lanes), axis=1)
                            term = on * ref[c].astype(jnp.float32)
                            total = term if total is None else total + term
                    blocks.append(total)
                out[d, b] = jnp.concatenate(blocks, axis=0).astype(jnp.bfloat16)


def residual_kernel(targets, parts, z_half, rows, *refs):
    t_refs = refs[: parts * targets]
    right, occupied, virtual, out = refs[parts * targets :]
    z, y, core, _ = place()
    right_tiles, _, _, depth = t_refs[0].shape
    low = lax.rem(z, parts)
    for d in range(right_tiles):
        cols = slice(d * TILE, (d + 1) * TILE)
        total = None
        for q in range(targets // 2):
            for b in range(2):
                pieces = [
                    t_refs[(o ^ (q % parts)) * targets + 2 * q + rel_y][d, b]
                    for o in range(parts)
                    for rel_y in range(2)
                ]
                start = pl.multiple_of((z ^ q ^ (b * z_half)) * depth, depth)
                term = jnp.dot(
                    jnp.concatenate(pieces, axis=0),
                    right[pl.ds(start, depth), cols],
                    preferred_element_type=jnp.float32,
                )
                total = term if total is None else total + term
        source = 0
        for o in range(parts):
            for rel_y in range(2):
                for rel in range(2):
                    at = (((low ^ o) * 2 + (y ^ rel_y)) * 2 + (core ^ rel)) * rows
                    at = pl.multiple_of(at, rows)
                    shift = occupied[pl.ds(at, rows), :] + virtual[:, cols]
                    out[pl.ds(at, rows), cols] = total[source : source + rows, :] / shift
                    source += rows


def solution(mesh):
    tiles, inner_size = mesh.shape["tile"], mesh.shape["inner"]
    z_size, chips = tiles // 4, tiles // 2
    parts, half, z_half = z_size // inner_size, chips // 2, z_size // 2

    def swap(value, q, axis="tile", size=tiles):
        return lax.ppermute(value, axis, [(t, t ^ q) for t in range(size)])

    def cross(value, p):
        pairs = [
            (t * inner_size + n, (t ^ (4 * z_half)) * inner_size + (n ^ p))
            for t in range(tiles)
            for n in range(inner_size)
        ]
        return lax.ppermute(value, ("tile", "inner"), pairs)

    def call(kernel, operands, in_specs, out_shape, scratch=(), flops=0, moved=1 << 20):
        many = isinstance(out_shape, list)
        return pl.pallas_call(
            kernel,
            out_shape=out_shape,
            in_specs=in_specs,
            out_specs=[VMEM] * len(out_shape) if many else VMEM,
            scratch_shapes=list(scratch),
            compiler_params=PARAMS,
            cost_estimate=cost(flops, moved),
        )(*operands)

    def on_device(amplitudes, left_factors, right_factors, tile_pattern, occupied_shift, virtual_shift):
        rows, width = amplitudes.shape
        block = left_factors.shape[0]
        out_width = right_factors.shape[1]
        left_tiles, right_tiles = width // TILE, out_width // TILE
        depth = 4 * block

        lanes = min(128, depth)
        on = (tile_pattern != 0).astype(jnp.float32)
        mask = jnp.broadcast_to(on[:, :, None], (*tile_pattern.shape, lanes))
        kept = call(
            keep_kernel, (amplitudes, left_factors), [VMEM] * 2, pltpu.VMEM((rows + block, width), amplitudes.dtype)
        )
        by_y = swap(left_factors, 2)
        lefts = [swap(left_factors, 1), by_y, swap(by_y, 1)]
        amps = {q: swap(amplitudes, 4 * q) for q in range(1, z_half + 1)}
        amps |= {q: swap(amps[z_half], 4 * (q ^ z_half)) for q in range(z_half + 1, z_size)}

        packed = jnp.bfloat16 if rows % 16 == 0 else jnp.float32
        scratch = [
            pltpu.VMEM((inner_size * rows, width), packed),
            pltpu.VMEM((inner_size * rows, depth), jnp.float32),
        ]
        shapes = [
            jax.ShapeDtypeStruct((left_tiles, rows, depth), kind)
            for _ in range(inner_size)
            for kind in (jnp.float32, jnp.bfloat16)
        ]
        flops = 2 * inner_size * rows * width * depth
        arrived = []
        for s in range(parts):
            blocks = [amps[r * parts + s] for r in range(inner_size) if r or s]
            if s == 0:
                *products, left_all = call(
                    functools.partial(first_products_kernel, inner_size, parts),
                    (kept, *blocks, *lefts),
                    [VMEM] * (inner_size + 3),
                    shapes + [pltpu.VMEM((depth, width), jnp.bfloat16)],
                    scratch,
                    flops,
                )
            else:
                products = call(
                    functools.partial(next_products_kernel, inner_size, parts),
                    (*blocks, left_all),
                    [VMEM] * (inner_size + 1),
                    shapes,
                    scratch,
                    flops,
                )
            crossed = [cross(products[2 * p + 1], p) for p in range(inner_size)]
            mine = [products[0]]
            mine += [swap(products[2 * p], p, "inner", inner_size) for p in range(1, inner_size)]
            other = [swap(part, 1) for part in mine]
            crossed_other = [swap(part, 1) for part in crossed]
            operands = (mask, *mine, *other, *crossed, *crossed_other)
            made = call(
                functools.partial(totals_kernel, inner_size, right_tiles),
                operands,
                [VMEM] * len(operands),
                [jax.ShapeDtypeStruct((right_tiles, 2, 2 * rows, depth), jnp.bfloat16)] * half,
            )
            arrived += [made[0]] + [swap(made[m], 2 * m) for m in range(1, half)]

        return call(
            functools.partial(residual_kernel, half, parts, z_half, rows),
            (*arrived, right_factors, occupied_shift.reshape(-1, 1), virtual_shift.reshape(1, -1)),
            [VMEM] * (len(arrived) + 3),
            jax.ShapeDtypeStruct((occupied_shift.shape[0], out_width), jnp.float32),
            (),
            2 * occupied_shift.shape[0] * out_width * right_factors.shape[0],
            4 << 20,
        )


    placed = (P("tile", "inner"), P("tile", "inner"), P(None, "tile"), P(), P("inner"), P("tile"))
    return jax.shard_map(on_device, mesh=mesh, in_specs=placed, out_specs=P("inner", "tile"), check_vma=False)
```

```python
import functools

import jax
import jax.numpy as jnp
from jax import lax
from jax.experimental import pallas as pl
from jax.experimental.pallas import tpu as pltpu
from jax.sharding import PartitionSpec as P


TILE = 512
VMEM = pl.BlockSpec(memory_space=pltpu.VMEM)
SMEM = pl.BlockSpec(memory_space=pltpu.SMEM)
ANY = pl.BlockSpec(memory_space=pl.ANY)
PARAMS = pltpu.CompilerParams(vmem_limit_bytes=20 * 1024 * 1024)


def cost(flops, moved):
    return pl.CostEstimate(flops=int(flops), bytes_accessed=int(moved), transcendentals=0)


def keep_kernel(amplitudes, left, kept):
    rows = amplitudes.shape[0]
    kept[:rows, :] = amplitudes[...]
    kept[rows:, :] = left[...]


def place():
    t = lax.axis_index("tile")
    return t // 4, lax.rem(t // 2, 2), lax.rem(t, 2), lax.axis_index("inner")


def multiply(parts, a_refs, l_all, outs, a_all, result):
    z, _, _, inner = place()
    rows, width = a_refs[0].shape
    for r, ref in enumerate(a_refs):
        a_all[r * rows : (r + 1) * rows, :] = ref[...].astype(a_all.dtype)
    for c in range(width // TILE):
        cols = slice(c * TILE, (c + 1) * TILE)
        result[...] = lax.dot_general(
            a_all[:, cols].astype(jnp.bfloat16),
            l_all[:, cols],
            (((1,), (1,)), ((), ())),
            preferred_element_type=jnp.float32,
        )
        for p in range(len(outs) // 2):
            start = pl.multiple_of((inner ^ p ^ (z // parts)) * rows, rows)
            value = result[pl.ds(start, rows), :]
            outs[2 * p][c] = value
            outs[2 * p + 1][c] = value.astype(jnp.bfloat16)


def first_products_kernel(inner_size, parts, kept, *refs):
    a_refs, l_refs = refs[: inner_size - 1], refs[inner_size - 1 : inner_size + 2]
    outs = refs[inner_size + 2 : 3 * inner_size + 2]
    l_all, a_all, result = refs[3 * inner_size + 2 :]
    _, y, core, _ = place()
    block = l_refs[0].shape[0]
    rows = kept.shape[0] - block
    for q, ref in enumerate((kept.at[rows:, :],) + l_refs):
        where = ((y ^ (q // 2)) * 2 + (core ^ (q % 2))) * block
        l_all[pl.ds(pl.multiple_of(where, block), block), :] = ref[...]
    multiply(parts, (kept.at[:rows, :],) + a_refs, l_all, outs, a_all, result)


def next_products_kernel(inner_size, parts, *refs):
    a_refs, l_all = refs[:inner_size], refs[inner_size]
    outs = refs[inner_size + 1 : 3 * inner_size + 1]
    a_all, result = refs[3 * inner_size + 1 :]
    multiply(parts, a_refs, l_all, outs, a_all, result)


def weights_kernel(inner_size, left_tiles, right_tiles, targets, rows, mask, out):
    z, y, core, inner = place()
    chip = z * 2 + y
    count = inner_size * left_tiles
    lanes = mask.shape[2]
    lane = lax.broadcasted_iota(jnp.int32, (rows, count * rows), 1)
    diagonal = lax.rem(lane, rows) == lax.broadcasted_iota(jnp.int32, (rows, count * rows), 0)
    block = lane // rows
    for m in range(targets):
        for d in range(right_tiles):
            column = ((chip ^ m) * 2 + core) * right_tiles + d
            value = jnp.zeros((rows, count * rows), jnp.float32)
            for i in range(count):
                row = (inner ^ (i // left_tiles)) * left_tiles + i % left_tiles
                on = mask[row, pl.ds(column, 1), :]
                value = jnp.where(block == i, jnp.concatenate([on] * (count * rows // lanes), axis=1), value)
            at = (m * right_tiles + d) * rows
            out[at : at + rows, :] = jnp.where(diagonal, value, 0.0).astype(jnp.bfloat16)


def totals_kernel(inner_size, right_tiles, weights, *refs):
    count = 4 * inner_size
    sources, outs = refs[:count], refs[count:]
    left_tiles, rows, depth = sources[0].shape
    shape = (left_tiles * rows, depth)
    for b in range(2):
        for rel in range(2):
            high, low = [], []
            for p in range(inner_size):
                ref = sources[(b * 2 + rel) * inner_size + p]
                value = ref[...]
                if ref.dtype == jnp.float32 or rows % 16:
                    value = value.astype(jnp.float32).reshape(shape)
                    rounded = value.astype(jnp.bfloat16)
                    low.append((value - rounded.astype(jnp.float32)).astype(jnp.bfloat16))
                    value = rounded
                high.append(value.reshape(shape))
            total = jnp.dot(weights[...], jnp.concatenate(high, axis=0), preferred_element_type=jnp.float32)
            if b == 0:
                total += jnp.dot(weights[...], jnp.concatenate(low, axis=0), preferred_element_type=jnp.float32)
            for m, out in enumerate(outs):
                for d in range(right_tiles):
                    at = (m * right_tiles + d) * rows
                    out[d, b, rel * rows : (rel + 1) * rows, :] = total[at : at + rows, :].astype(jnp.bfloat16)


def inverse_kernel(occupied, virtual, out):
    lanes = 128
    column = jnp.broadcast_to(occupied[...], (lanes, out.shape[0])).T
    for at in range(0, out.shape[1], lanes):
        out[:, at : at + lanes] = 1.0 / (column + virtual[:, at : at + lanes])


def residual_kernel(targets, parts, z_half, rows, *refs):
    t_refs = refs[: parts * targets]
    right, inverse, out, staged, left, sem = refs[parts * targets :]
    z, y, core, _ = place()
    right_tiles, _, _, depth = t_refs[0].shape
    low = lax.rem(z, parts)
    for d in range(right_tiles):
        cols = slice(d * TILE, (d + 1) * TILE)
        total = None
        for q in range(targets // 2):
            for b in range(2):
                pieces = [
                    t_refs[(o ^ (q % parts)) * targets + 2 * q + rel_y][d, b]
                    for o in range(parts)
                    for rel_y in range(2)
                ]
                at = pl.ds(pl.multiple_of((z ^ q ^ (b * z_half)) * depth, depth), depth)
                if depth % 128 == 0:
                    for i, piece in enumerate(pieces):
                        left[d, i * 2 * rows : (i + 1) * 2 * rows, at] = piece
                else:
                    piece = jnp.concatenate(pieces, axis=0)
                    term = jnp.dot(piece, right[at, cols], preferred_element_type=jnp.float32)
                    total = term if total is None else total + term
        if depth % 128 == 0:
            total = jnp.dot(left[d], right[:, cols], preferred_element_type=jnp.float32)
        source = 0
        for o in range(parts):
            for rel_y in range(2):
                for rel in range(2):
                    at = (((low ^ o) * 2 + (y ^ rel_y)) * 2 + (core ^ rel)) * rows
                    at = pl.multiple_of(at, rows)
                    scale = inverse[pl.ds(at, rows), cols]
                    staged[pl.ds(at, rows), cols] = total[source : source + rows, :] * scale
                    source += rows
        pltpu.make_async_copy(staged.at[:, cols], out.at[:, cols], sem.at[d]).start()
    for d in range(right_tiles):
        cols = slice(d * TILE, (d + 1) * TILE)
        pltpu.make_async_copy(staged.at[:, cols], out.at[:, cols], sem.at[d]).wait()


def solution(mesh):
    tiles, inner_size = mesh.shape["tile"], mesh.shape["inner"]
    z_size, chips = tiles // 4, tiles // 2
    parts, half, z_half = z_size // inner_size, chips // 2, z_size // 2

    def swap(value, q, axis="tile", size=tiles):
        return lax.ppermute(value, axis, [(t, t ^ q) for t in range(size)])

    def cross(value, p):
        pairs = [
            (t * inner_size + n, (t ^ (4 * z_half)) * inner_size + (n ^ p))
            for t in range(tiles)
            for n in range(inner_size)
        ]
        return lax.ppermute(value, ("tile", "inner"), pairs)

    def call(name, kernel, operands, in_specs, out_shape, scratch=(), flops=0, moved=1 << 20):
        many = isinstance(out_shape, list)
        return pl.pallas_call(
            kernel,
            out_shape=out_shape,
            in_specs=in_specs,
            out_specs=[VMEM] * len(out_shape) if many else ANY if name == "residual" else VMEM,
            scratch_shapes=list(scratch),
            compiler_params=PARAMS,
            cost_estimate=cost(flops, moved),
        )(*operands)

    def on_device(amplitudes, left_factors, right_factors, tile_pattern, occupied_shift, virtual_shift):
        rows, width = amplitudes.shape
        block = left_factors.shape[0]
        out_width = right_factors.shape[1]
        left_tiles, right_tiles = width // TILE, out_width // TILE
        depth = 4 * block

        lanes = min(128, depth)
        on = (tile_pattern != 0).astype(jnp.float32)
        mask = jnp.broadcast_to(on[:, :, None], (*tile_pattern.shape, lanes))
        weights = call(
            "weights",
            functools.partial(weights_kernel, inner_size, left_tiles, right_tiles, half, rows),
            (mask,),
            [VMEM],
            pltpu.VMEM((half * right_tiles * rows, inner_size * left_tiles * rows), jnp.bfloat16),
        )
        kept = call(
            "keep",
            keep_kernel,
            (amplitudes, left_factors),
            [VMEM] * 2,
            pltpu.VMEM((rows + block, width), amplitudes.dtype),
        )
        by_y = swap(left_factors, 2)
        lefts = [swap(left_factors, 1), by_y, swap(by_y, 1)]
        amps = {q: swap(amplitudes, 4 * q) for q in range(1, z_half + 1)}
        amps |= {q: swap(amps[z_half], 4 * (q ^ z_half)) for q in range(z_half + 1, z_size)}

        packed = jnp.bfloat16 if rows % 16 == 0 else jnp.float32
        scratch = [
            pltpu.VMEM((inner_size * rows, width), packed),
            pltpu.VMEM((inner_size * rows, depth), jnp.float32),
        ]
        shapes = [
            pltpu.VMEM((left_tiles, rows, depth), kind)
            for _ in range(inner_size)
            for kind in (jnp.float32, jnp.bfloat16)
        ]
        flops = 2 * inner_size * rows * width * depth
        arrived = []
        for s in range(parts):
            blocks = [amps[r * parts + s] for r in range(inner_size) if r or s]
            if s == 0:
                *products, left_all = call(
                    "products0",
                    functools.partial(first_products_kernel, inner_size, parts),
                    (kept, *blocks, *lefts),
                    [VMEM] * (inner_size + 3),
                    shapes + [pltpu.VMEM((depth, width), jnp.bfloat16)],
                    scratch,
                    flops,
                )
            else:
                products = call(
                    f"products{s}",
                    functools.partial(next_products_kernel, inner_size, parts),
                    (*blocks, left_all),
                    [VMEM] * (inner_size + 1),
                    shapes,
                    scratch,
                    flops,
                )
            crossed = [cross(products[2 * p + 1], p) for p in range(inner_size)]
            mine = [products[0]]
            mine += [swap(products[2 * p], p, "inner", inner_size) for p in range(1, inner_size)]
            other = [swap(part, 1) for part in mine]
            crossed_other = [swap(part, 1) for part in crossed]
            operands = (weights, *mine, *other, *crossed, *crossed_other)
            made = call(
                f"totals{s}",
                functools.partial(totals_kernel, inner_size, right_tiles),
                operands,
                [VMEM] * len(operands),
                [pltpu.VMEM((right_tiles, 2, 2 * rows, depth), jnp.bfloat16)] * half,
            )
            arrived += [made[0]] + [swap(made[m], 2 * m) for m in range(1, half)]

        result_shape = (occupied_shift.shape[0], out_width)
        inverse = call(
            "inverse",
            inverse_kernel,
            (occupied_shift.reshape(1, -1), virtual_shift.reshape(1, -1)),
            [VMEM] * 2,
            pltpu.VMEM(result_shape, jnp.float32),
        )
        return call(
            "residual",
            functools.partial(residual_kernel, half, parts, z_half, rows),
            (*arrived, right_factors, inverse),
            [VMEM] * (len(arrived) + 2),
            jax.ShapeDtypeStruct(result_shape, jnp.float32),
            [
                pltpu.VMEM(result_shape, jnp.float32),
                pltpu.VMEM((right_tiles, result_shape[0], right_factors.shape[0]), jnp.bfloat16),
                pltpu.SemaphoreType.DMA((right_tiles,)),
            ],
            2 * occupied_shift.shape[0] * out_width * right_factors.shape[0],
            4 << 20,
        )


    placed = (P("tile", "inner"), P("tile", "inner"), P(None, "tile"), P(), P("inner"), P("tile"))
    return jax.shard_map(on_device, mesh=mesh, in_specs=placed, out_specs=P("inner", "tile"), check_vma=False)
```

```python
import functools

import jax
import jax.numpy as jnp
from jax import lax
from jax.experimental import pallas as pl
from jax.experimental.pallas import tpu as pltpu
from jax.sharding import PartitionSpec as P


TILE = 512
VMEM = pl.BlockSpec(memory_space=pltpu.VMEM)
SMEM = pl.BlockSpec(memory_space=pltpu.SMEM)
ANY = pl.BlockSpec(memory_space=pl.ANY)
PARAMS = pltpu.CompilerParams(vmem_limit_bytes=20 * 1024 * 1024)


def cost(flops, moved):
    return pl.CostEstimate(flops=int(flops), bytes_accessed=int(moved), transcendentals=0)


def keep_kernel(amplitudes, left, kept):
    rows = amplitudes.shape[0]
    kept[:rows, :] = amplitudes[...]
    kept[rows:, :] = left[...]


def place():
    t = lax.axis_index("tile")
    return t // 4, lax.rem(t // 2, 2), lax.rem(t, 2), lax.axis_index("inner")


def multiply(parts, a_refs, l_all, outs, a_all, result):
    z, _, _, inner = place()
    rows, width = a_refs[0].shape
    for r, ref in enumerate(a_refs):
        a_all[r * rows : (r + 1) * rows, :] = ref[...].astype(a_all.dtype)
    for c in range(width // TILE):
        cols = slice(c * TILE, (c + 1) * TILE)
        result[...] = lax.dot_general(
            a_all[:, cols].astype(jnp.bfloat16),
            l_all[:, cols],
            (((1,), (1,)), ((), ())),
            preferred_element_type=jnp.float32,
        )
        for p in range(len(outs) // 2):
            start = pl.multiple_of((inner ^ p ^ (z // parts)) * rows, rows)
            value = result[pl.ds(start, rows), :]
            outs[2 * p][c] = value
            outs[2 * p + 1][c] = value.astype(jnp.bfloat16)


def first_products_kernel(inner_size, parts, kept, *refs):
    a_refs, l_refs = refs[: inner_size - 1], refs[inner_size - 1 : inner_size + 2]
    outs = refs[inner_size + 2 : 3 * inner_size + 2]
    l_all, a_all, result = refs[3 * inner_size + 2 :]
    _, y, core, _ = place()
    block = l_refs[0].shape[0]
    rows = kept.shape[0] - block
    for q, ref in enumerate((kept.at[rows:, :],) + l_refs):
        where = ((y ^ (q // 2)) * 2 + (core ^ (q % 2))) * block
        l_all[pl.ds(pl.multiple_of(where, block), block), :] = ref[...]
    multiply(parts, (kept.at[:rows, :],) + a_refs, l_all, outs, a_all, result)


def next_products_kernel(inner_size, parts, *refs):
    a_refs, l_all = refs[:inner_size], refs[inner_size]
    outs = refs[inner_size + 1 : 3 * inner_size + 1]
    a_all, result = refs[3 * inner_size + 1 :]
    multiply(parts, a_refs, l_all, outs, a_all, result)


def weights_kernel(inner_size, left_tiles, right_tiles, targets, rows, mask, out):
    z, y, core, inner = place()
    chip = z * 2 + y
    count = inner_size * left_tiles
    lanes = mask.shape[2]
    lane = lax.broadcasted_iota(jnp.int32, (rows, count * rows), 1)
    diagonal = lax.rem(lane, rows) == lax.broadcasted_iota(jnp.int32, (rows, count * rows), 0)
    block = lane // rows
    for m in range(targets):
        for d in range(right_tiles):
            column = ((chip ^ m) * 2 + core) * right_tiles + d
            value = jnp.zeros((rows, count * rows), jnp.float32)
            for i in range(count):
                row = (inner ^ (i // left_tiles)) * left_tiles + i % left_tiles
                on = mask[row, pl.ds(column, 1), :]
                value = jnp.where(block == i, jnp.concatenate([on] * (count * rows // lanes), axis=1), value)
            at = (m * right_tiles + d) * rows
            out[at : at + rows, :] = jnp.where(diagonal, value, 0.0).astype(jnp.bfloat16)


def totals_kernel(inner_size, right_tiles, weights, *refs):
    count = 4 * inner_size
    sources, outs = refs[:count], refs[count:]
    left_tiles, rows, depth = sources[0].shape
    shape = (left_tiles * rows, depth)
    for b in range(2):
        for rel in range(2):
            high, low = [], []
            for p in range(inner_size):
                ref = sources[(b * 2 + rel) * inner_size + p]
                value = ref[...]
                if ref.dtype == jnp.float32 or rows % 16:
                    value = value.astype(jnp.float32).reshape(shape)
                    rounded = value.astype(jnp.bfloat16)
                    low.append((value - rounded.astype(jnp.float32)).astype(jnp.bfloat16))
                    value = rounded
                high.append(value.reshape(shape))
            total = jnp.dot(weights[...], jnp.concatenate(high, axis=0), preferred_element_type=jnp.float32)
            if b == 0:
                total += jnp.dot(weights[...], jnp.concatenate(low, axis=0), preferred_element_type=jnp.float32)
            for m, out in enumerate(outs):
                for d in range(right_tiles):
                    at = (m * right_tiles + d) * rows
                    out[d, b, rel * rows : (rel + 1) * rows, :] = total[at : at + rows, :].astype(jnp.bfloat16)


def inverse_kernel(occupied, virtual, out):
    lanes = 128
    column = jnp.broadcast_to(occupied[...], (lanes, out.shape[0])).T
    for at in range(0, out.shape[1], lanes):
        out[:, at : at + lanes] = 1.0 / (column + virtual[:, at : at + lanes])


def gather_kernel(parts, part, last, z_half, *refs):
    targets = 4 * z_half // 2
    t_refs, right, rest = refs[:targets], refs[targets], refs[targets + 1 :]
    so_far, rest = (rest[0], rest[1:]) if part else (None, rest)
    if last:
        inverse, out, staged, sem = rest
    else:
        (out,) = rest
    z, y, core, _ = place()
    right_tiles, _, both, depth = t_refs[0].shape
    low, rows = lax.rem(z, parts), both // 2
    for d in range(right_tiles):
        cols = slice(d * TILE, (d + 1) * TILE)
        for o in range(parts):
            here = slice(o * 2 * both, (o + 1) * 2 * both)
            total = None if so_far is None else so_far[here, cols]
            for q in range(targets // 2):
                if q % parts != o ^ part:
                    continue
                for b in range(2):
                    left = jnp.concatenate([t_refs[2 * q][d, b], t_refs[2 * q + 1][d, b]], axis=0)
                    at = pl.ds(pl.multiple_of((z ^ q ^ (b * z_half)) * depth, depth), depth)
                    term = jnp.dot(left, right[at, cols], preferred_element_type=jnp.float32)
                    total = term if total is None else total + term
            if not last:
                out[here, cols] = total
                continue
            for i in range(4):
                at = (((low ^ o) * 2 + (y ^ (i // 2))) * 2 + (core ^ (i % 2))) * rows
                at = pl.ds(pl.multiple_of(at, rows), rows)
                staged[at, cols] = total[i * rows : (i + 1) * rows, :] * inverse[at, cols]
        if last:
            pltpu.make_async_copy(staged.at[:, cols], out.at[:, cols], sem.at[d]).start()
    if last:
        for d in range(right_tiles):
            cols = slice(d * TILE, (d + 1) * TILE)
            pltpu.make_async_copy(staged.at[:, cols], out.at[:, cols], sem.at[d]).wait()


def solution(mesh):
    tiles, inner_size = mesh.shape["tile"], mesh.shape["inner"]
    z_size, chips = tiles // 4, tiles // 2
    parts, half, z_half = z_size // inner_size, chips // 2, z_size // 2

    def swap(value, q, axis="tile", size=tiles):
        return lax.ppermute(value, axis, [(t, t ^ q) for t in range(size)])

    def cross(value, p):
        pairs = [
            (t * inner_size + n, (t ^ (4 * z_half)) * inner_size + (n ^ p))
            for t in range(tiles)
            for n in range(inner_size)
        ]
        return lax.ppermute(value, ("tile", "inner"), pairs)

    def call(name, kernel, operands, in_specs, out_shape, scratch=(), flops=0, moved=1 << 20):
        many = isinstance(out_shape, list)
        return pl.pallas_call(
            kernel,
            out_shape=out_shape,
            in_specs=in_specs,
            out_specs=[VMEM] * len(out_shape) if many else ANY if name == "residual" else VMEM,
            scratch_shapes=list(scratch),
            compiler_params=PARAMS,
            cost_estimate=cost(flops, moved),
        )(*operands)

    def on_device(amplitudes, left_factors, right_factors, tile_pattern, occupied_shift, virtual_shift):
        rows, width = amplitudes.shape
        block = left_factors.shape[0]
        out_width = right_factors.shape[1]
        left_tiles, right_tiles = width // TILE, out_width // TILE
        depth = 4 * block

        lanes = min(128, depth)
        on = (tile_pattern != 0).astype(jnp.float32)
        mask = jnp.broadcast_to(on[:, :, None], (*tile_pattern.shape, lanes))
        weights = call(
            "weights",
            functools.partial(weights_kernel, inner_size, left_tiles, right_tiles, half, rows),
            (mask,),
            [VMEM],
            pltpu.VMEM((half * right_tiles * rows, inner_size * left_tiles * rows), jnp.bfloat16),
        )
        kept = call(
            "keep",
            keep_kernel,
            (amplitudes, left_factors),
            [VMEM] * 2,
            pltpu.VMEM((rows + block, width), amplitudes.dtype),
        )
        by_y = swap(left_factors, 2)
        lefts = [swap(left_factors, 1), by_y, swap(by_y, 1)]
        amps = {q: swap(amplitudes, 4 * q) for q in range(1, z_half + 1)}
        amps |= {q: swap(amps[z_half], 4 * (q ^ z_half)) for q in range(z_half + 1, z_size)}

        packed = jnp.bfloat16 if rows % 16 == 0 else jnp.float32
        scratch = [
            pltpu.VMEM((inner_size * rows, width), packed),
            pltpu.VMEM((inner_size * rows, depth), jnp.float32),
        ]
        shapes = [
            pltpu.VMEM((left_tiles, rows, depth), kind)
            for _ in range(inner_size)
            for kind in (jnp.float32, jnp.bfloat16)
        ]
        flops = 2 * inner_size * rows * width * depth
        arrived = []
        for s in range(parts):
            blocks = [amps[r * parts + s] for r in range(inner_size) if r or s]
            if s == 0:
                *products, left_all = call(
                    "products0",
                    functools.partial(first_products_kernel, inner_size, parts),
                    (kept, *blocks, *lefts),
                    [VMEM] * (inner_size + 3),
                    shapes + [pltpu.VMEM((depth, width), jnp.bfloat16)],
                    scratch,
                    flops,
                )
            else:
                products = call(
                    f"products{s}",
                    functools.partial(next_products_kernel, inner_size, parts),
                    (*blocks, left_all),
                    [VMEM] * (inner_size + 1),
                    shapes,
                    scratch,
                    flops,
                )
            crossed = [cross(products[2 * p + 1], p) for p in range(inner_size)]
            mine = [products[0]]
            mine += [swap(products[2 * p], p, "inner", inner_size) for p in range(1, inner_size)]
            other = [swap(part, 1) for part in mine]
            crossed_other = [swap(part, 1) for part in crossed]
            operands = (weights, *mine, *other, *crossed, *crossed_other)
            made = call(
                f"totals{s}",
                functools.partial(totals_kernel, inner_size, right_tiles),
                operands,
                [VMEM] * len(operands),
                [pltpu.VMEM((right_tiles, 2, 2 * rows, depth), jnp.bfloat16)] * half,
            )
            arrived.append([made[0]] + [swap(made[m], 2 * m) for m in range(1, half)])

        result_shape = (occupied_shift.shape[0], out_width)
        inverse = call(
            "inverse",
            inverse_kernel,
            (occupied_shift.reshape(1, -1), virtual_shift.reshape(1, -1)),
            [VMEM] * 2,
            pltpu.VMEM(result_shape, jnp.float32),
        )
        sums = ()
        for s in range(parts):
            last = s == parts - 1
            operands = (*arrived[s], right_factors, *sums) + ((inverse,) if last else ())
            sums = (
                call(
                    "residual" if last else f"sums{s}",
                    functools.partial(gather_kernel, parts, s, last, z_half),
                    operands,
                    [VMEM] * len(operands),
                    jax.ShapeDtypeStruct(result_shape, jnp.float32) if last else pltpu.VMEM(result_shape, jnp.float32),
                    [pltpu.VMEM(result_shape, jnp.float32), pltpu.SemaphoreType.DMA((right_tiles,))] if last else (),
                    2 * occupied_shift.shape[0] * out_width * right_factors.shape[0] // parts,
                    4 << 20,
                ),
            )
        return sums[0]


    placed = (P("tile", "inner"), P("tile", "inner"), P(None, "tile"), P(), P("inner"), P("tile"))
    return jax.shard_map(on_device, mesh=mesh, in_specs=placed, out_specs=P("inner", "tile"), check_vma=False)
```

```python
import functools

import jax
import jax.numpy as jnp
from jax import lax
from jax.experimental import pallas as pl
from jax.experimental.pallas import tpu as pltpu
from jax.sharding import PartitionSpec as P


TILE = 512
VMEM = pl.BlockSpec(memory_space=pltpu.VMEM)
SMEM = pl.BlockSpec(memory_space=pltpu.SMEM)
ANY = pl.BlockSpec(memory_space=pl.ANY)
PARAMS = pltpu.CompilerParams(vmem_limit_bytes=20 * 1024 * 1024)


def cost(flops, moved):
    return pl.CostEstimate(flops=int(flops), bytes_accessed=int(moved), transcendentals=0)


def keep_kernel(amplitudes, left, kept):
    rows = amplitudes.shape[0]
    kept[:rows, :] = amplitudes[...]
    kept[rows:, :] = left[...]


def place():
    t = lax.axis_index("tile")
    return t // 4, lax.rem(t // 2, 2), lax.rem(t, 2), lax.axis_index("inner")


def multiply(parts, a_refs, l_all, outs, a_all, result):
    z, _, _, inner = place()
    rows, width = a_refs[0].shape
    for r, ref in enumerate(a_refs):
        a_all[r * rows : (r + 1) * rows, :] = ref[...].astype(a_all.dtype)
    for c in range(width // TILE):
        cols = slice(c * TILE, (c + 1) * TILE)
        result[...] = lax.dot_general(
            a_all[:, cols].astype(jnp.bfloat16),
            l_all[:, cols],
            (((1,), (1,)), ((), ())),
            preferred_element_type=jnp.float32,
        )
        for p in range(len(outs) // 2):
            start = pl.multiple_of((inner ^ p ^ (z // parts)) * rows, rows)
            value = result[pl.ds(start, rows), :]
            outs[2 * p][c] = value
            outs[2 * p + 1][c] = value.astype(jnp.bfloat16)


def first_products_kernel(inner_size, parts, kept, *refs):
    a_refs, l_refs = refs[: inner_size - 1], refs[inner_size - 1 : inner_size + 2]
    outs = refs[inner_size + 2 : 3 * inner_size + 2]
    l_all, a_all, result = refs[3 * inner_size + 2 :]
    _, y, core, _ = place()
    block = l_refs[0].shape[0]
    rows = kept.shape[0] - block
    for q, ref in enumerate((kept.at[rows:, :],) + l_refs):
        where = ((y ^ (q // 2)) * 2 + (core ^ (q % 2))) * block
        l_all[pl.ds(pl.multiple_of(where, block), block), :] = ref[...]
    multiply(parts, (kept.at[:rows, :],) + a_refs, l_all, outs, a_all, result)


def next_products_kernel(inner_size, parts, *refs):
    a_refs, l_all = refs[:inner_size], refs[inner_size]
    outs = refs[inner_size + 1 : 3 * inner_size + 1]
    a_all, result = refs[3 * inner_size + 1 :]
    multiply(parts, a_refs, l_all, outs, a_all, result)


def weights_kernel(inner_size, left_tiles, right_tiles, targets, rows, mask, out):
    z, y, core, inner = place()
    chip = z * 2 + y
    count = inner_size * left_tiles
    lanes = mask.shape[2]
    lane = lax.broadcasted_iota(jnp.int32, (rows, count * rows), 1)
    diagonal = lax.rem(lane, rows) == lax.broadcasted_iota(jnp.int32, (rows, count * rows), 0)
    block = lane // rows
    for m in range(targets):
        for d in range(right_tiles):
            column = ((chip ^ m) * 2 + core) * right_tiles + d
            value = jnp.zeros((rows, count * rows), jnp.float32)
            for i in range(count):
                row = (inner ^ (i // left_tiles)) * left_tiles + i % left_tiles
                on = mask[row, pl.ds(column, 1), :]
                value = jnp.where(block == i, jnp.concatenate([on] * (count * rows // lanes), axis=1), value)
            at = (m * right_tiles + d) * rows
            out[at : at + rows, :] = jnp.where(diagonal, value, 0.0).astype(jnp.bfloat16)


def totals_kernel(inner_size, right_tiles, weights, *refs):
    count = 4 * inner_size
    sources, outs = refs[:count], refs[count:]
    left_tiles, rows, depth = sources[0].shape
    shape = (left_tiles * rows, depth)
    for b in range(2):
        for rel in range(2):
            high, low = [], []
            for p in range(inner_size):
                ref = sources[(b * 2 + rel) * inner_size + p]
                value = ref[...]
                if ref.dtype == jnp.float32 or rows % 16:
                    value = value.astype(jnp.float32).reshape(shape)
                    rounded = value.astype(jnp.bfloat16)
                    low.append((value - rounded.astype(jnp.float32)).astype(jnp.bfloat16))
                    value = rounded
                high.append(value.reshape(shape))
            total = jnp.dot(weights[...], jnp.concatenate(high, axis=0), preferred_element_type=jnp.float32)
            if b == 0:
                total += jnp.dot(weights[...], jnp.concatenate(low, axis=0), preferred_element_type=jnp.float32)
            for m, out in enumerate(outs):
                for d in range(right_tiles):
                    at = (m * right_tiles + d) * rows
                    out[d, b, rel * rows : (rel + 1) * rows, :] = total[at : at + rows, :].astype(jnp.bfloat16)


def inverse_kernel(occupied, virtual, out):
    lanes = 128
    column = jnp.broadcast_to(occupied[...], (lanes, out.shape[0])).T
    for at in range(0, out.shape[1], lanes):
        out[:, at : at + lanes] = 1.0 / (column + virtual[:, at : at + lanes])


def gather_kernel(parts, part, last, z_half, *refs):
    targets = 4 * z_half // 2
    t_refs, right, rest = refs[:targets], refs[targets], refs[targets + 1 :]
    so_far, rest = (rest[0], rest[1:]) if part else (None, rest)
    if last:
        inverse, out, staged, sem = rest
    else:
        (out,) = rest
    z, y, core, _ = place()
    right_tiles, _, both, depth = t_refs[0].shape
    low, rows = lax.rem(z, parts), both // 2
    piece = TILE // 2
    for k in range(2 * right_tiles):
        d, cols = k // 2, slice(k * piece, (k + 1) * piece)
        for o in range(parts):
            here = slice(o * 2 * both, (o + 1) * 2 * both)
            total = None if so_far is None else so_far[here, cols]
            for q in range(targets // 2):
                if q % parts != o ^ part:
                    continue
                for b in range(2):
                    left = jnp.concatenate([t_refs[2 * q][d, b], t_refs[2 * q + 1][d, b]], axis=0)
                    at = pl.ds(pl.multiple_of((z ^ q ^ (b * z_half)) * depth, depth), depth)
                    term = jnp.dot(left, right[at, cols], preferred_element_type=jnp.float32)
                    total = term if total is None else total + term
            if not last:
                out[here, cols] = total
                continue
            for i in range(4):
                at = (((low ^ o) * 2 + (y ^ (i // 2))) * 2 + (core ^ (i % 2))) * rows
                at = pl.ds(pl.multiple_of(at, rows), rows)
                staged[at, cols] = total[i * rows : (i + 1) * rows, :] * inverse[at, cols]
        if last:
            pltpu.make_async_copy(staged.at[:, cols], out.at[:, cols], sem.at[k]).start()
    if last:
        for k in range(2 * right_tiles):
            cols = slice(k * piece, (k + 1) * piece)
            pltpu.make_async_copy(staged.at[:, cols], out.at[:, cols], sem.at[k]).wait()


def solution(mesh):
    tiles, inner_size = mesh.shape["tile"], mesh.shape["inner"]
    z_size, chips = tiles // 4, tiles // 2
    parts, half, z_half = z_size // inner_size, chips // 2, z_size // 2

    def swap(value, q, axis="tile", size=tiles):
        return lax.ppermute(value, axis, [(t, t ^ q) for t in range(size)])

    def cross(value, p):
        pairs = [
            (t * inner_size + n, (t ^ (4 * z_half)) * inner_size + (n ^ p))
            for t in range(tiles)
            for n in range(inner_size)
        ]
        return lax.ppermute(value, ("tile", "inner"), pairs)

    def call(name, kernel, operands, in_specs, out_shape, scratch=(), flops=0, moved=1 << 20):
        many = isinstance(out_shape, list)
        return pl.pallas_call(
            kernel,
            out_shape=out_shape,
            in_specs=in_specs,
            out_specs=[VMEM] * len(out_shape) if many else ANY if name == "residual" else VMEM,
            scratch_shapes=list(scratch),
            compiler_params=PARAMS,
            cost_estimate=cost(flops, moved),
        )(*operands)

    def on_device(amplitudes, left_factors, right_factors, tile_pattern, occupied_shift, virtual_shift):
        rows, width = amplitudes.shape
        block = left_factors.shape[0]
        out_width = right_factors.shape[1]
        left_tiles, right_tiles = width // TILE, out_width // TILE
        depth = 4 * block

        lanes = min(128, depth)
        on = (tile_pattern != 0).astype(jnp.float32)
        mask = jnp.broadcast_to(on[:, :, None], (*tile_pattern.shape, lanes))
        weights = call(
            "weights",
            functools.partial(weights_kernel, inner_size, left_tiles, right_tiles, half, rows),
            (mask,),
            [VMEM],
            pltpu.VMEM((half * right_tiles * rows, inner_size * left_tiles * rows), jnp.bfloat16),
        )
        kept = call(
            "keep",
            keep_kernel,
            (amplitudes, left_factors),
            [VMEM] * 2,
            pltpu.VMEM((rows + block, width), amplitudes.dtype),
        )
        by_y = swap(left_factors, 2)
        lefts = [swap(left_factors, 1), by_y, swap(by_y, 1)]
        amps = {q: swap(amplitudes, 4 * q) for q in range(1, z_half + 1)}
        amps |= {q: swap(amps[z_half], 4 * (q ^ z_half)) for q in range(z_half + 1, z_size)}

        packed = jnp.bfloat16 if rows % 16 == 0 else jnp.float32
        scratch = [
            pltpu.VMEM((inner_size * rows, width), packed),
            pltpu.VMEM((inner_size * rows, depth), jnp.float32),
        ]
        shapes = [
            pltpu.VMEM((left_tiles, rows, depth), kind)
            for _ in range(inner_size)
            for kind in (jnp.float32, jnp.bfloat16)
        ]
        flops = 2 * inner_size * rows * width * depth
        arrived = []
        for s in range(parts):
            blocks = [amps[r * parts + s] for r in range(inner_size) if r or s]
            if s == 0:
                *products, left_all = call(
                    "products0",
                    functools.partial(first_products_kernel, inner_size, parts),
                    (kept, *blocks, *lefts),
                    [VMEM] * (inner_size + 3),
                    shapes + [pltpu.VMEM((depth, width), jnp.bfloat16)],
                    scratch,
                    flops,
                )
            else:
                products = call(
                    f"products{s}",
                    functools.partial(next_products_kernel, inner_size, parts),
                    (*blocks, left_all),
                    [VMEM] * (inner_size + 1),
                    shapes,
                    scratch,
                    flops,
                )
            crossed = [cross(products[2 * p + 1], p) for p in range(inner_size)]
            mine = [products[0]]
            mine += [swap(products[2 * p], p, "inner", inner_size) for p in range(1, inner_size)]
            other = [swap(part, 1) for part in mine]
            crossed_other = [swap(part, 1) for part in crossed]
            operands = (weights, *mine, *other, *crossed, *crossed_other)
            made = call(
                f"totals{s}",
                functools.partial(totals_kernel, inner_size, right_tiles),
                operands,
                [VMEM] * len(operands),
                [pltpu.VMEM((right_tiles, 2, 2 * rows, depth), jnp.bfloat16)] * half,
            )
            arrived.append([made[0]] + [swap(made[m], 2 * m) for m in range(1, half)])

        result_shape = (occupied_shift.shape[0], out_width)
        inverse = call(
            "inverse",
            inverse_kernel,
            (occupied_shift.reshape(1, -1), virtual_shift.reshape(1, -1)),
            [VMEM] * 2,
            pltpu.VMEM(result_shape, jnp.float32),
        )
        sums = ()
        for s in range(parts):
            last = s == parts - 1
            operands = (*arrived[s], right_factors, *sums) + ((inverse,) if last else ())
            sums = (
                call(
                    "residual" if last else f"sums{s}",
                    functools.partial(gather_kernel, parts, s, last, z_half),
                    operands,
                    [VMEM] * len(operands),
                    jax.ShapeDtypeStruct(result_shape, jnp.float32) if last else pltpu.VMEM(result_shape, jnp.float32),
                    [pltpu.VMEM(result_shape, jnp.float32), pltpu.SemaphoreType.DMA((2 * right_tiles,))] if last else (),
                    2 * occupied_shift.shape[0] * out_width * right_factors.shape[0] // parts,
                    4 << 20,
                ),
            )
        return sums[0]


    placed = (P("tile", "inner"), P("tile", "inner"), P(None, "tile"), P(), P("inner"), P("tile"))
    return jax.shard_map(on_device, mesh=mesh, in_specs=placed, out_specs=P("inner", "tile"), check_vma=False)
```
